512 devices in a mesh: section: 4 (over x), tm: 2 (over core), space: 64 (over y, z).
Axes of the slice: x: 4, y: 8, z: 8, core: 2. Of those that a mesh axis runs over, the one named last changes fastest.
Arguments:
- video: bfloat16 [4, 512, 128, 128], P('tm', ('section', 'space')), may hold values from -6 to 6
- cotangent: bfloat16 [4, 512, 128, 128], P('tm', ('section', 'space')), may hold values from -6 to 6
- spatial_weights: bfloat16 [4, 9, 128, 128], P('section'), may hold values from -0.1875 to 0.1875
- temporal_weights: bfloat16 [4, 3, 128, 128], P('section'), may hold values from -0.3125 to 0.3125
Outputs:
- grad_spatial: float32 [4, 9, 128, 128], P('section')
- grad_temporal: float32 [4, 3, 128, 128], P('section')
- grad_video: bfloat16 [4, 512, 128, 128], P('tm', ('section', 'space'))
The draws below stay inside these ranges and needn't reach their ends.
All inputs are finite; a program needn't handle non-finite values.
Results may differ from the reference program's by a relative error of at most 0.019.
Values may be sent and summed in bfloat16 or wider, within the bound.
A program may use at most 64 MiB of HBM per device.

```python
import jax
import jax.numpy as jnp

C = 128
W = 128
FRAMES = 4
H = 512
SECTIONS = 4


def block_scale(key, dims, shards, smallest, top_value):
    factor_of = 1.0
    for dim, blocks in shards:
        steps = jax.random.uniform(jax.random.fold_in(jax.random.fold_in(key, 6), dim), (blocks,), jnp.float32, smallest / len(shards), top_value / len(shards))
        factor_of = factor_of * jnp.repeat(jnp.exp(steps), dims[dim] // blocks).reshape((-1,) + (1,) * (len(dims) - 1 - dim))
    return factor_of


def normal_values(key, extent, deviation, most, pieces=(), dtype=jnp.bfloat16):
    loudness = block_scale(key, extent, pieces, -0.22, 0.18) if pieces else 1.0
    array = jax.random.normal(key, extent, jnp.float32) * deviation * loudness
    return jnp.minimum(jnp.maximum(array, -most), most).astype(dtype)


def setup_inputs(seed: int = 0) -> dict:
    splits = jax.random.split(jax.random.key(seed), 5)
    return {
        "video": normal_values(splits[0], (FRAMES, H, W, C), 1.0, 6.0, ((0, 2), (1, 256))),
        "cotangent": normal_values(splits[1], (FRAMES, H, W, C), 1.0, 6.0, ((0, 2), (1, 256))),
        "spatial_weights": normal_values(splits[2], (SECTIONS, 9, C, C), (9 * C) ** -0.5, 0.1875, ((0, 4),)),
        "temporal_weights": normal_values(splits[3], (SECTIONS, 3, C, C), (3 * C) ** -0.5, 0.3125, ((0, 4),)),
    }


def conv_forward(inputs, spatial_weight, temporal_weight):
    frames, height, columns, chans = inputs.shape
    padded = jnp.pad(inputs.astype(jnp.float32), ((0, 0), (1, 1), (1, 1), (0, 0)))
    before = jnp.zeros((frames, height, columns, chans), jnp.float32)
    for offset in range(9):
        row_off = offset // 3
        col_off = offset % 3
        before = before + jnp.einsum('frwc,cd->frwd', padded[:, row_off:row_off + height, col_off:col_off + columns], spatial_weight[offset].astype(jnp.float32))
    hidden = jax.nn.silu(before).astype(jnp.bfloat16)
    timeline = jnp.pad(hidden.astype(jnp.float32), ((2, 0), (0, 0), (0, 0), (0, 0)))
    mixed = jnp.zeros((frames, height, columns, chans), jnp.float32)
    for offset in range(3):
        mixed = mixed + jnp.einsum('frwc,cd->frwd', timeline[offset:offset + frames], temporal_weight[offset].astype(jnp.float32))
    outputs = (inputs.astype(jnp.float32) + mixed).astype(jnp.bfloat16)
    return (padded, before, timeline, outputs)

def conv_backward(grad, padded, before, timeline, spatial_weight, temporal_weight):
    frames, height, columns, chans = grad.shape
    grad_f = grad.astype(jnp.float32)
    ahead = jnp.pad(grad_f, ((0, 2), (0, 0), (0, 0), (0, 0)))
    temporal_list = []
    hidden_grad = jnp.zeros((frames, height, columns, chans), jnp.float32)
    for offset in range(3):
        temporal_list.append(jnp.einsum('frwc,frwd->cd', timeline[offset:offset + frames], grad_f))
        hidden_grad = hidden_grad + jnp.einsum('frwd,cd->frwc', ahead[2 - offset:2 - offset + frames], temporal_weight[offset].astype(jnp.float32))
    sigma = jax.nn.sigmoid(before)
    pre_grad = (hidden_grad * sigma * (1.0 + before * (1.0 - sigma))).astype(jnp.bfloat16)
    pre_f = pre_grad.astype(jnp.float32)
    rimmed = jnp.pad(pre_f, ((0, 0), (1, 1), (1, 1), (0, 0)))
    spatial_list = []
    back = jnp.zeros((frames, height, columns, chans), jnp.float32)
    for offset in range(9):
        row_off = offset // 3
        col_off = offset % 3
        spatial_list.append(jnp.einsum('frwc,frwd->cd', padded[:, row_off:row_off + height, col_off:col_off + columns], pre_f))
        back = back + jnp.einsum('frwd,cd->frwc', rimmed[:, 2 - row_off:2 - row_off + height, 2 - col_off:2 - col_off + columns], spatial_weight[offset].astype(jnp.float32))
    new_grad = (grad_f + back).astype(jnp.bfloat16)
    return (jnp.stack(spatial_list), jnp.stack(temporal_list), new_grad)

def reference(video, cotangent, spatial_weights, temporal_weights):
    blocks = spatial_weights.shape[0]
    records = []
    inputs = video
    for step in range(blocks):
        padded, before, timeline, outputs = conv_forward(inputs, spatial_weights[step], temporal_weights[step])
        records.append((padded, before, timeline))
        inputs = outputs
    grad = cotangent
    spatial_out = [None] * blocks
    temporal_out = [None] * blocks
    for step in reversed(range(blocks)):
        padded, before, timeline = records[step]
        spatial_grad, temporal_grad, grad = conv_backward(grad, padded, before, timeline, spatial_weights[step], temporal_weights[step])
        spatial_out[step] = spatial_grad
        temporal_out[step] = temporal_grad
    factor = 1.0 / math_sqrt(cotangent.shape[0] * cotangent.shape[1] * cotangent.shape[2])
    return (jnp.stack(spatial_out) * factor, jnp.stack(temporal_out) * factor, grad)

def math_sqrt(count):
    return float(count) ** 0.5
```

```python
import functools

import jax
import jax.numpy as jnp
from jax import lax
from jax.experimental import pallas as pl
from jax.experimental.pallas import tpu as pltpu
from jax.sharding import PartitionSpec as P

MESH = pl.DeviceIdType.MESH
F32 = jnp.float32
BF16 = jnp.bfloat16
C = 128


def nn(a, b):
    return jnp.dot(a, b, preferred_element_type=F32)


def nt(a, b):
    return lax.dot_general(a, b, (((1,), (1,)), ((), ())), preferred_element_type=F32)


def tn(a, b):
    return lax.dot_general(a, b, (((0,), (0,)), ((), ())), preferred_element_type=F32)


def from_left(v):
    column = lax.broadcasted_iota(jnp.int32, v.shape, 0)
    return jnp.where(column == 0, 0.0, pltpu.roll(v, 1, 0))


def from_right(v):
    column = lax.broadcasted_iota(jnp.int32, v.shape, 0)
    last = v.shape[0] - 1
    return jnp.where(column == last, 0.0, pltpu.roll(v, last, 0))


def flat(v):
    return v.reshape(-1, v.shape[-1])


def side(a, b):
    return jnp.concatenate([flat(a), flat(b)], axis=1)


def kernel(
    nx, ny, nz, factor,
    video, cotangent, sw, tw,
    gout, gvid,
    xs, dcoef, hs, hp, gs, gl, das, da3, yacc, tacc,
    wr, wk, wb, town, tprev,
    gb, rb, r1s, r1r, r2t, r2s, r2r, r3s, r3r, ag1, ag2,
    s_x, s_d, s_h, s_g, s_w, s_f, s_c, s_y, s_z, s_r, s_az, s_ay, s_ac,
):
    blocks = nx
    space = ny * nz
    x = lax.axis_index("section")
    c = lax.axis_index("tm")
    sp = lax.axis_index("space")
    y = sp // nz
    z = sp % nz
    line = x * space + sp
    total = nx * space
    up = (line + total - 1) % total
    down = (line + 1) % total
    dev_up = (up // space, c, up % space)
    dev_down = (down // space, c, down % space)
    other = 1 - c
    partner = (x, other, sp)
    rows1 = r1s.shape[2]
    rows2 = r2s.shape[2]
    half = C // 2
    mine = pl.ds(pl.multiple_of(c * half, half), half)

    def at_x(d):
        return ((x + d) % nx, c, sp)

    def at_y(d):
        return (x, c, ((y + d) % ny) * nz + z)

    def at_z(d):
        return (x, c, y * nz + (z + d) % nz)

    def remote(src, dst, sems, device):
        return pltpu.make_async_remote_copy(
            src_ref=src, dst_ref=dst, send_sem=sems.at[0], recv_sem=sems.at[1],
            device_id=device, device_id_type=MESH,
        )

    def each(lo, hi, body):
        def step(i, carry):
            body(i)
            return carry
        lax.fori_loop(lo, hi, step, 0)

    def halo_x(s):
        return (
            remote(xs.at[s, 1], xs.at[s, 3], s_x.at[s, 0], dev_up),
            remote(xs.at[s, 2], xs.at[s, 0], s_x.at[s, 1], dev_down),
        )

    def halo_d(s):
        return (
            remote(das.at[s, 1], das.at[s, 3], s_d.at[s, 0], dev_up),
            remote(das.at[s, 2], das.at[s, 0], s_d.at[s, 1], dev_down),
        )

    def copy_h(s):
        return remote(hs.at[s], hp.at[s], s_h.at[s], partner)

    def copy_g(s):
        return remote(gs.at[s], gl.at[s], s_g.at[s], partner)

    def copy_w(d):
        return (
            remote(sw.at[0, :, mine], wr.at[x, pl.ds(0, 9), mine], s_w.at[d, 0], at_x(d)),
            remote(tw.at[0, :, mine], wr.at[x, pl.ds(9, 3), mine], s_w.at[d, 1], at_x(d)),
        )

    def copy_f(b):
        return remote(wr.at[b, :, mine], wr.at[b, :, mine], s_f.at[b], partner)

    def copy_c(s):
        return remote(gb.at[s, other], rb.at[s], s_c.at[s], partner)

    def copy_y(s, d):
        return remote(r1s.at[s, (y + d) % ny], r1r.at[s, d], s_y.at[s, d], at_y(d))

    def copy_z(s, d):
        return remote(r2s.at[s, (z + d) % nz], r2r.at[s, d], s_z.at[s, d], at_z(d))

    def copy_r(s):
        d = (s + nx - x) % nx
        return remote(r3s.at[s], r3r.at[d], s_r.at[d], (s, c, sp))

    def copy_az(d):
        return remote(ag1.at[z], ag1.at[z], s_az.at[d], at_z(d))

    def copy_ay(d):
        return remote(ag2.at[c, y], ag2.at[c, y], s_ay.at[d], at_y(d))

    def copy_ac(d):
        j = (y + ny - d) % ny
        return remote(ag2.at[c, j], ag2.at[c, j], s_ac.at[d], partner)

    barrier = pltpu.get_barrier_semaphore()
    peers = [dev_up, dev_down, partner]
    peers += [at_x(d) for d in range(1, nx)]
    peers += [at_y(d) for d in range(1, ny)]
    peers += [at_z(d) for d in range(1, nz)]
    for peer in peers:
        pl.semaphore_signal(barrier, inc=1, device_id=peer, device_id_type=MESH)

    for f in range(2):
        for r in range(2):
            xs[0, 1 + r, f] = video[f, r]
    gs[blocks] = cotangent[...]
    wr[x, 0:9] = sw[0]
    wr[x, 9:12] = tw[0]

    @pl.when(c == 0)
    def _():
        hp[...] = jnp.zeros_like(hp)

    pl.semaphore_wait(barrier, len(peers))

    def send_weights(owner):
        @pl.when(x == owner)
        def _():
            for d in range(1, nx):
                for copy in copy_w(d):
                    copy.start()

    def forward_weights(b):
        @pl.when(x != b)
        def _():
            d = (x + nx - b) % nx
            for copy in copy_w(d):
                copy.wait_recv()
            copy_f(b).start()

    send_weights(0)
    for copy in halo_x(0):
        copy.start()
    send_weights(1)

    @pl.when(c == 1)
    def _():
        copy_g(blocks).start()

    forward_weights(0)

    def zero_edges(ref, s):
        @pl.when(line == 0)
        def _():
            ref[s, 0] = jnp.zeros(ref.shape[2:], ref.dtype)

        @pl.when(line == total - 1)
        def _():
            ref[s, 3] = jnp.zeros(ref.shape[2:], ref.dtype)

    def forward(s):
        @pl.when(x != s)
        def _():
            copy_f(s).wait_recv()

        for ky in range(3):
            for kx in range(3):
                tap = wr[s, 3 * ky + kx]
                wk[s, ky * C:(ky + 1) * C, kx * C:(kx + 1) * C] = tap
                wb[s, kx * C:(kx + 1) * C, (2 - ky) * C:(3 - ky) * C] = tap
        zero = jnp.zeros((C, C), BF16)
        town[s, 0:C, 0:C] = wr[s, 11]
        town[s, 0:C, C:2 * C] = wr[s, 10]
        town[s, C:2 * C, 0:C] = zero
        town[s, C:2 * C, C:2 * C] = wr[s, 11]
        tprev[s, 0:C, 0:C] = wr[s, 9]
        tprev[s, 0:C, C:2 * C] = zero
        tprev[s, C:2 * C, 0:C] = wr[s, 10]
        tprev[s, C:2 * C, C:2 * C] = wr[s, 9]

        own = side(xs[s, 1], xs[s, 2])
        yacc[0] = nn(own, wk[s, C:3 * C])
        yacc[1] = nn(own, wk[s, 0:2 * C])
        for copy in halo_x(s):
            copy.wait_recv()
        zero_edges(xs, s)
        for r in range(2):
            rim = flat(xs[s, 3 * r])
            full = yacc[r] + nn(rim, wk[s, 2 * r * C:(2 * r + 1) * C])
            for f in range(2):
                part = full[f * C:(f + 1) * C]
                pre = (
                    from_left(part[:, 0:C]) + part[:, C:2 * C] + from_right(part[:, 2 * C:3 * C])
                )
                sig = 0.5 * jnp.tanh(0.5 * pre) + 0.5
                hs[s, f, r] = (pre * sig).astype(BF16)
                dcoef[s, r, f] = sig * (1.0 + pre * (1.0 - sig))

        @pl.when(c == 0)
        def _():
            copy_h(s).start()

        @pl.when(s < blocks - 1)
        def _():
            tacc[...] = nn(side(hs[s, 0], hs[s, 1]), town[s])

        @pl.when(c == 1)
        def _():
            copy_h(s).wait_recv()

        @pl.when(s < blocks - 1)
        def _():
            @pl.when(c == 1)
            def _():
                tacc[...] += nn(side(hp[s, 0], hp[s, 1]), tprev[s])

            for r in range(2):
                for f in range(2):
                    mix = tacc[r * C:(r + 1) * C, f * C:(f + 1) * C]
                    xs[s + 1, 1 + r, f] = (xs[s, 1 + r, f].astype(F32) + mix).astype(BF16)
            for copy in halo_x(s + 1):
                copy.start()
            for owner in range(2, nx):
                @pl.when(s == owner - 2)
                def _():
                    send_weights(owner)
            forward_weights(s + 1)

    each(0, blocks, forward)

    def core_sum(s):
        copy_c(s).wait_recv()
        for j in range(ny):
            rows = slice(j * rows1, (j + 1) * rows1)
            r1s[s, j] = (gb[s, c, rows].astype(F32) + rb[s, rows].astype(F32)).astype(BF16)
        each(1, ny, lambda d: copy_y(s, d).start())

    def y_sum(s):
        each(1, ny, lambda d: copy_y(s, d).wait_recv())
        part = r1s[s, y].astype(F32)
        for d in range(1, ny):
            part = part + r1r[s, d].astype(F32)
        r2t[...] = part
        for j in range(nz):
            r2s[s, j] = r2t[j * rows2:(j + 1) * rows2]
        each(1, nz, lambda d: copy_z(s, d).start())

    def z_sum(s):
        each(1, nz, lambda d: copy_z(s, d).wait_recv())
        part = r2s[s, z]
        for d in range(1, nz):
            part = part + r2r[s, d]
        r3s[s] = part

        @pl.when(x != s)
        def _():
            copy_r(s).start()

    def backward(step):
        s = blocks - 1 - step
        grad = side(gs[s + 1, 0], gs[s + 1, 1])
        tacc[...] = nt(grad, town[s])

        @pl.when(c == 0)
        def _():
            copy_g(s + 1).wait_recv()
            tacc[...] += nt(side(gl[s + 1, 0], gl[s + 1, 1]), tprev[s])

        for r in range(2):
            for f in range(2):
                da = tacc[r * C:(r + 1) * C, f * C:(f + 1) * C] * dcoef[s, r, f]
                das[s, 1 + r, f] = da.astype(BF16)
        for copy in halo_d(s):
            copy.start()

        own = side(das[s, 1], das[s, 2])
        yacc[0] = nt(own, wb[s, :, C:3 * C])
        yacc[1] = nt(own, wb[s, :, 0:2 * C])

        for r in range(2):
            for f in range(2):
                da = das[s, 1 + r, f].astype(F32)
                da3[r, f * C:(f + 1) * C, 0:C] = from_right(da).astype(BF16)
                da3[r, f * C:(f + 1) * C, C:2 * C] = das[s, 1 + r, f]
                da3[r, f * C:(f + 1) * C, 2 * C:3 * C] = from_left(da).astype(BF16)
        grad = side(gs[s + 1, 0], gs[s + 1, 1])
        outer = tn(
            jnp.concatenate(
                [flat(hp[s, 0]), flat(hp[s, 1]), flat(hs[s, 0]), flat(hs[s, 1])], axis=1
            ),
            grad,
        )
        for kt in range(3):
            gt = outer[kt * C:(kt + 1) * C, 0:C] + outer[(kt + 1) * C:(kt + 2) * C, C:2 * C]
            gb[s, 1, (3 + kt) * C:(4 + kt) * C] = gt.astype(BF16)
        for ky in range(3):
            gw = tn(flat(xs[s, ky:ky + 2]), flat(da3[...]))
            for kx in range(3):
                tap = 3 * ky + kx
                row = (tap % 6) * C
                gb[s, tap // 6, row:row + C] = gw[:, kx * C:(kx + 1) * C].astype(BF16)
        copy_c(s).start()

        @pl.when(s < blocks - 1)
        def _():
            y_sum(s + 1)

        @pl.when(s < blocks - 2)
        def _():
            z_sum(s + 2)

        for copy in halo_d(s):
            copy.wait_recv()
        zero_edges(das, s)
        for r in range(2):
            rim = flat(das[s, 3 * r])
            full = yacc[r] + nt(rim, wb[s, :, 2 * r * C:(2 * r + 1) * C])
            for f in range(2):
                part = full[f * C:(f + 1) * C]
                back = (
                    from_right(part[:, 0:C]) + part[:, C:2 * C] + from_left(part[:, 2 * C:3 * C])
                )
                gs[s, f, r] = (gs[s + 1, f, r].astype(F32) + back).astype(BF16)

        @pl.when((c == 1) & (s > 0))
        def _():
            copy_g(s).start()

        core_sum(s)

    each(0, blocks, backward)

    y_sum(0)
    gvid[...] = gs[0]
    if blocks > 1:
        z_sum(1)
    z_sum(0)

    part = r3s[x]
    for d in range(1, nx):
        pltpu_wait = remote(r3s.at[0], r3r.at[d], s_r.at[d], at_x(d))
        pltpu_wait.wait_recv()
        part = part + r3r[d]
    ag1[z] = part * factor
    each(1, nz, lambda d: copy_az(d).start())
    each(1, nz, lambda d: copy_az(d).wait_recv())
    for j in range(nz):
        r2t[j * rows2:(j + 1) * rows2] = ag1[j]
    ag2[c, y] = r2t[...].astype(BF16)
    each(1, ny, lambda d: copy_ay(d).start())
    copy_ac(0).start()

    def hand_on(d):
        copy_ay(d).wait_recv()
        copy_ac(d).start()

    each(1, ny, hand_on)
    each(0, ny, lambda d: copy_ac(d).wait_recv())
    gout[...] = ag2[...]

    def sent(s):
        for copy in halo_x(s) + halo_d(s):
            copy.wait_send()
        copy_c(s).wait_send()
        each(1, ny, lambda d: copy_y(s, d).wait_send())
        each(1, nz, lambda d: copy_z(s, d).wait_send())

        @pl.when(x != s)
        def _():
            copy_r(s).wait_send()
            copy_f(s).wait_send()

        @pl.when(c == 0)
        def _():
            copy_h(s).wait_send()

        @pl.when(c == 1)
        def _():
            copy_g(s + 1).wait_send()

    each(0, blocks, sent)
    for d in range(1, nx):
        for copy in copy_w(d):
            copy.wait_send()
    each(1, nz, lambda d: copy_az(d).wait_send())
    each(1, ny, lambda d: copy_ay(d).wait_send())
    each(0, ny, lambda d: copy_ac(d).wait_send())


def on_device(nx, ny, nz, pixels, video, cotangent, spatial_weights, temporal_weights):
    blocks = nx
    tile = (2, 2, C, C)
    rows = 6 * C
    rows1 = rows // ny
    rows2 = rows1 // nz
    vmem = pltpu.VMEM
    dma = pltpu.SemaphoreType.DMA
    scratch = [
        vmem((blocks, 4, 2, C, C), BF16),
        vmem((blocks,) + tile, F32),
        vmem((blocks,) + tile, BF16),
        vmem((blocks,) + tile, BF16),
        vmem((blocks + 1,) + tile, BF16),
        vmem((blocks + 1,) + tile, BF16),
        vmem((blocks, 4, 2, C, C), BF16),
        vmem((2, 2 * C, 3 * C), BF16),
        vmem((2, 2 * C, 3 * C), F32),
        vmem((2 * C, 2 * C), F32),
        vmem((blocks, 12, C, C), BF16),
        vmem((blocks, 3 * C, 3 * C), BF16),
        vmem((blocks, 3 * C, 3 * C), BF16),
        vmem((blocks, 2 * C, 2 * C), BF16),
        vmem((blocks, 2 * C, 2 * C), BF16),
        vmem((blocks, 2, rows, C), BF16),
        vmem((blocks, rows, C), BF16),
        vmem((blocks, ny, rows1, C), BF16),
        vmem((blocks, ny, rows1, C), BF16),
        vmem((rows1, C), F32),
        vmem((blocks, nz, rows2, C), F32),
        vmem((blocks, nz, rows2, C), F32),
        vmem((blocks, rows2, C), F32),
        vmem((nx, rows2, C), F32),
        vmem((nz, rows2, C), F32),
        vmem((2, ny, rows1, C), BF16),
        dma((blocks, 2, 2)),
        dma((blocks, 2, 2)),
        dma((blocks, 2)),
        dma((blocks + 1, 2)),
        dma((nx, 2, 2)),
        dma((nx, 2)),
        dma((blocks, 2)),
        dma((blocks, ny, 2)),
        dma((blocks, nz, 2)),
        dma((nx, 2)),
        dma((nz, 2)),
        dma((ny, 2)),
        dma((ny, 2)),
    ]
    grads, grad_video = pl.pallas_call(
        functools.partial(kernel, nx, ny, nz, 1.0 / float(pixels) ** 0.5),
        out_shape=(
            jax.ShapeDtypeStruct((2, ny, rows1, C), BF16),
            jax.ShapeDtypeStruct(tile, BF16),
        ),
        in_specs=[pl.BlockSpec(memory_space=vmem)] * 4,
        out_specs=(pl.BlockSpec(memory_space=vmem),) * 2,
        scratch_shapes=scratch,
        compiler_params=pltpu.CompilerParams(
            collective_id=0, has_side_effects=True, vmem_limit_bytes=40 << 20
        ),
    )(video, cotangent, spatial_weights, temporal_weights)
    grads = grads.reshape(1, 12, C, C).astype(F32)
    return grads[:, :9], grads[:, 9:], grad_video


def solution(mesh):
    nx = mesh.shape["section"]
    space = mesh.shape["space"]
    nz = 1 << ((space.bit_length() - 1 + 1) // 2)
    ny = space // nz
    frames = 2 * mesh.shape["tm"]
    height = 2 * nx * space
    pixels = frames * height * C
    tiles = P("tm", ("section", "space"), None, None)
    owned = P("section", None, None, None)
    return jax.shard_map(
        functools.partial(on_device, nx, ny, nz, pixels),
        mesh=mesh,
        in_specs=(tiles, tiles, owned, owned),
        out_specs=(owned, owned, tiles),
        check_vma=False,
    )
```

```python
import functools

import jax
import jax.numpy as jnp
from jax import lax
from jax.experimental import pallas as pl
from jax.experimental.pallas import tpu as pltpu
from jax.sharding import PartitionSpec as P

MESH = pl.DeviceIdType.MESH
F32 = jnp.float32
BF16 = jnp.bfloat16
C = 128


def nn(a, b):
    return jnp.dot(a, b, preferred_element_type=F32)


def nt(a, b):
    return lax.dot_general(a, b, (((1,), (1,)), ((), ())), preferred_element_type=F32)


def tn(a, b):
    return lax.dot_general(a, b, (((0,), (0,)), ((), ())), preferred_element_type=F32)


def from_left(v):
    column = lax.broadcasted_iota(jnp.int32, v.shape, 0)
    return jnp.where(column == 0, 0.0, pltpu.roll(v, 1, 0))


def from_right(v):
    column = lax.broadcasted_iota(jnp.int32, v.shape, 0)
    last = v.shape[0] - 1
    return jnp.where(column == last, 0.0, pltpu.roll(v, last, 0))


def flat(v):
    return v.reshape(-1, v.shape[-1])


def side(a, b):
    return jnp.concatenate([flat(a), flat(b)], axis=1)


def kernel(
    nx, ny, nz, factor,
    video, cotangent, sw, tw,
    gout, gvid,
    xs, dcoef, hs, hp, gs, gl, das, da3, yacc, tacc,
    wr, wk, wb, town, tprev,
    gb, rb, r1s, r1r, r2t, r2s, r3r, ag1, ag2,
    s_in, s_x, s_d, s_h, s_g, s_w, s_f, s_c, s_a, s_b, s_bg, s_ag, s_ac,
):
    blocks = nx
    space = ny * nz
    x = lax.axis_index("section")
    c = lax.axis_index("tm")
    sp = lax.axis_index("space")
    y = sp // nz
    z = sp % nz
    line = x * space + sp
    total = nx * space
    up = (line + total - 1) % total
    down = (line + 1) % total
    dev_up = (up // space, c, up % space)
    dev_down = (down // space, c, down % space)
    other = 1 - c
    partner = (x, other, sp)
    rows1 = r1s.shape[2]
    na = r1s.shape[1]
    nb = r2s.shape[1]
    rows2 = rows1 // nb
    ia = y * (1 - c) + z * c
    ib = z * (1 - c) + y * c
    half = C // 2
    mine = pl.ds(pl.multiple_of(c * half, half), half)

    def at_x(d):
        return ((x + d) % nx, c, sp)

    def at_a(d):
        return (x, c, ((y + d * (1 - c)) % ny) * nz + (z + d * c) % nz)

    def at_b(d, owner):
        return (owner, c, ((y + d * c) % ny) * nz + (z + d * (1 - c)) % nz)

    def remote(src, dst, sems, device):
        return pltpu.make_async_remote_copy(
            src_ref=src, dst_ref=dst, send_sem=sems.at[0], recv_sem=sems.at[1],
            device_id=device, device_id_type=MESH,
        )

    def each(lo, hi, body):
        def step(i, carry):
            body(i)
            return carry
        lax.fori_loop(lo, hi, step, 0)

    def halo_x(s):
        return (
            remote(xs.at[s, 1], xs.at[s, 3], s_x.at[s, 0], dev_up),
            remote(xs.at[s, 2], xs.at[s, 0], s_x.at[s, 1], dev_down),
        )

    def halo_d(s):
        return (
            remote(das.at[s, 1], das.at[s, 3], s_d.at[s, 0], dev_up),
            remote(das.at[s, 2], das.at[s, 0], s_d.at[s, 1], dev_down),
        )

    def copy_h(s):
        return remote(hs.at[s], hp.at[s], s_h.at[s], partner)

    def copy_g(s):
        return remote(gs.at[s], gl.at[s], s_g.at[s], partner)

    def copy_w(d):
        return remote(wr.at[x, :, mine], wr.at[x, :, mine], s_w.at[d], at_x(d))

    def copy_f(b):
        return remote(wr.at[b, :, mine], wr.at[b, :, mine], s_f.at[b], partner)

    def copy_c(s):
        return remote(gb.at[s, other], rb.at[s], s_c.at[s], partner)

    def copy_a(s, d):
        return remote(r1s.at[s, (ia + d) % na], r1r.at[s, d], s_a.at[s], at_a(d))

    def all_a(s):
        part = slice(1, na)
        return remote(r1s.at[s, part], r1r.at[s, part], s_a.at[s], at_a(1))

    def copy_b(s, d):
        slot = ((s + nx - x) % nx) * nb + d
        return remote(r2s.at[s, (ib + d) % nb], r3r.at[slot], s_b.at[s], at_b(d, s))

    def copy_bg(d):
        return remote(ag1.at[ib], ag1.at[ib], s_bg, at_b(d, x))

    def all_bg():
        part = ag1.at[slice(1, nb)]
        return remote(part, part, s_bg, at_b(1, x))

    def copy_ag(d):
        return remote(ag2.at[c, ia], ag2.at[c, ia], s_ag.at[d], at_a(d))

    def copy_ac(d):
        j = (ia + na - d) % na
        return remote(ag2.at[c, j], ag2.at[c, j], s_ac, partner)

    def all_ac():
        return remote(ag2.at[c], ag2.at[c], s_ac, partner)

    loads = [
        pltpu.make_async_copy(sw.at[0], wr.at[x, pl.ds(0, 9)], s_in.at[0]),
        pltpu.make_async_copy(tw.at[0], wr.at[x, pl.ds(9, 3)], s_in.at[1]),
        pltpu.make_async_copy(video.at[:, 0], xs.at[0, 1], s_in.at[2]),
        pltpu.make_async_copy(video.at[:, 1], xs.at[0, 2], s_in.at[3]),
        pltpu.make_async_copy(cotangent, gs.at[blocks], s_in.at[4]),
    ]
    for load in loads:
        load.start()

    barrier = pltpu.get_barrier_semaphore()
    peers = [dev_up, dev_down, partner]
    peers += [at_x(d) for d in range(1, nx)]
    peers += [at_a(d) for d in range(1, na)]
    peers += [at_b(d, (x + e) % nx) for e in range(nx) for d in range(1, nb)]
    for peer in peers:
        pl.semaphore_signal(barrier, inc=1, device_id=peer, device_id_type=MESH)

    @pl.when(c == 0)
    def _():
        hp[...] = jnp.zeros_like(hp)

    for load in loads:
        load.wait()
    pl.semaphore_wait(barrier, len(peers))

    def send_weights(owner):
        @pl.when(x == owner)
        def _():
            for d in range(1, nx):
                copy_w(d).start()

    def forward_weights(b):
        @pl.when(x != b)
        def _():
            d = (x + nx - b) % nx
            copy_w(d).wait_recv()
            copy_f(b).start()

    send_weights(0)
    for copy in halo_x(0):
        copy.start()
    send_weights(1)

    @pl.when(c == 1)
    def _():
        copy_g(blocks).start()

    forward_weights(0)

    def zero_edges(ref, s):
        @pl.when(line == 0)
        def _():
            ref[s, 0] = jnp.zeros(ref.shape[2:], ref.dtype)

        @pl.when(line == total - 1)
        def _():
            ref[s, 3] = jnp.zeros(ref.shape[2:], ref.dtype)

    def forward(s):
        @pl.when(x != s)
        def _():
            copy_f(s).wait_recv()

        for ky in range(3):
            for kx in range(3):
                tap = wr[s, 3 * ky + kx]
                wk[s, ky * C:(ky + 1) * C, kx * C:(kx + 1) * C] = tap
                wb[s, kx * C:(kx + 1) * C, (2 - ky) * C:(3 - ky) * C] = tap
        zero = jnp.zeros((C, C), BF16)
        town[s, 0:C, 0:C] = wr[s, 11]
        town[s, 0:C, C:2 * C] = wr[s, 10]
        town[s, C:2 * C, 0:C] = zero
        town[s, C:2 * C, C:2 * C] = wr[s, 11]
        tprev[s, 0:C, 0:C] = wr[s, 9]
        tprev[s, 0:C, C:2 * C] = zero
        tprev[s, C:2 * C, 0:C] = wr[s, 10]
        tprev[s, C:2 * C, C:2 * C] = wr[s, 9]

        own = side(xs[s, 1], xs[s, 2])
        yacc[0] = nn(own, wk[s, C:3 * C])
        yacc[1] = nn(own, wk[s, 0:2 * C])
        for copy in halo_x(s):
            copy.wait_recv()
        zero_edges(xs, s)
        for r in range(2):
            rim = flat(xs[s, 3 * r])
            full = yacc[r] + nn(rim, wk[s, 2 * r * C:(2 * r + 1) * C])
            for f in range(2):
                part = full[f * C:(f + 1) * C]
                pre = (
                    from_left(part[:, 0:C]) + part[:, C:2 * C] + from_right(part[:, 2 * C:3 * C])
                )
                sig = 0.5 * jnp.tanh(0.5 * pre) + 0.5
                hs[s, f, r] = (pre * sig).astype(BF16)
                dcoef[s, r, f] = sig * (1.0 + pre * (1.0 - sig))

        @pl.when(c == 0)
        def _():
            copy_h(s).start()

        @pl.when(s < blocks - 1)
        def _():
            tacc[...] = nn(side(hs[s, 0], hs[s, 1]), town[s])

        @pl.when(c == 1)
        def _():
            copy_h(s).wait_recv()

        @pl.when(s < blocks - 1)
        def _():
            @pl.when(c == 1)
            def _():
                tacc[...] += nn(side(hp[s, 0], hp[s, 1]), tprev[s])

            for r in range(2):
                for f in range(2):
                    mix = tacc[r * C:(r + 1) * C, f * C:(f + 1) * C]
                    xs[s + 1, 1 + r, f] = (xs[s, 1 + r, f].astype(F32) + mix).astype(BF16)
            for copy in halo_x(s + 1):
                copy.start()
            for owner in range(2, nx):
                @pl.when(s == owner - 2)
                def _():
                    send_weights(owner)
            forward_weights(s + 1)

    each(0, blocks, forward)

    def core_sum(s):
        copy_c(s).wait_recv()
        for j in range(na):
            rows = slice(j * rows1, (j + 1) * rows1)
            r1s[s, j] = (gb[s, c, rows].astype(F32) + rb[s, rows].astype(F32)).astype(BF16)
        each(1, na, lambda d: copy_a(s, d).start())

    def a_sum(s):
        all_a(s).wait_recv()
        part = r1s[s, ia].astype(F32)
        for d in range(1, na):
            part = part + r1r[s, d].astype(F32)
        r2t[...] = part
        for j in range(nb):
            r2s[s, j, 0:rows2] = r2t[j * rows2:(j + 1) * rows2]

        @pl.when(x == s)
        def _():
            r3r[0] = r2s[s, ib]

        @pl.when(x != s)
        def _():
            copy_b(s, 0).start()

        each(1, nb, lambda d: copy_b(s, d).start())

    def backward(step):
        s = blocks - 1 - step
        grad = side(gs[s + 1, 0], gs[s + 1, 1])
        tacc[...] = nt(grad, town[s])

        @pl.when(c == 0)
        def _():
            copy_g(s + 1).wait_recv()
            tacc[...] += nt(side(gl[s + 1, 0], gl[s + 1, 1]), tprev[s])

        for r in range(2):
            for f in range(2):
                da = tacc[r * C:(r + 1) * C, f * C:(f + 1) * C] * dcoef[s, r, f]
                das[s, 1 + r, f] = da.astype(BF16)
        for copy in halo_d(s):
            copy.start()

        own = side(das[s, 1], das[s, 2])
        yacc[0] = nt(own, wb[s, :, C:3 * C])
        yacc[1] = nt(own, wb[s, :, 0:2 * C])

        for r in range(2):
            for f in range(2):
                da = das[s, 1 + r, f].astype(F32)
                da3[r, f * C:(f + 1) * C, 0:C] = from_right(da).astype(BF16)
                da3[r, f * C:(f + 1) * C, C:2 * C] = das[s, 1 + r, f]
                da3[r, f * C:(f + 1) * C, 2 * C:3 * C] = from_left(da).astype(BF16)
        grad = side(gs[s + 1, 0], gs[s + 1, 1])
        outer = tn(
            jnp.concatenate(
                [flat(hp[s, 0]), flat(hp[s, 1]), flat(hs[s, 0]), flat(hs[s, 1])], axis=1
            ),
            grad,
        )
        for kt in range(3):
            gt = outer[kt * C:(kt + 1) * C, 0:C] + outer[(kt + 1) * C:(kt + 2) * C, C:2 * C]
            gb[s, 1, (3 + kt) * C:(4 + kt) * C] = gt.astype(BF16)
        for ky in range(3):
            gw = tn(flat(xs[s, ky:ky + 2]), flat(da3[...]))
            for kx in range(3):
                tap = 3 * ky + kx
                row = (tap % 6) * C
                gb[s, tap // 6, row:row + C] = gw[:, kx * C:(kx + 1) * C].astype(BF16)
        copy_c(s).start()

        @pl.when(s < blocks - 1)
        def _():
            a_sum(s + 1)

        for copy in halo_d(s):
            copy.wait_recv()
        zero_edges(das, s)
        for r in range(2):
            rim = flat(das[s, 3 * r])
            full = yacc[r] + nt(rim, wb[s, :, 2 * r * C:(2 * r + 1) * C])
            for f in range(2):
                part = full[f * C:(f + 1) * C]
                back = (
                    from_right(part[:, 0:C]) + part[:, C:2 * C] + from_left(part[:, 2 * C:3 * C])
                )
                gs[s, f, r] = (gs[s + 1, f, r].astype(F32) + back).astype(BF16)

        @pl.when((c == 1) & (s > 0))
        def _():
            copy_g(s).start()

        core_sum(s)

    each(0, blocks, backward)

    a_sum(0)
    gvid[...] = gs[0]

    others = slice(1, nx * nb)
    remote(r3r.at[others], r3r.at[others], s_b.at[x], at_b(1, x)).wait_recv()
    part = r3r[0]
    for d in range(1, nx * nb):
        part = part + r3r[d]
    ag1[ib] = part * factor
    each(1, nb, lambda d: copy_bg(d).start())
    all_bg().wait_recv()
    for j in range(nb):
        r2t[j * rows2:(j + 1) * rows2] = ag1[j, 0:rows2]
    ag2[c, ia] = r2t[...].astype(BF16)
    each(1, na, lambda d: copy_ag(d).start())
    copy_ac(0).start()

    def hand_on(d):
        copy_ag(d).wait_recv()
        copy_ac(d).start()

    each(1, na, hand_on)
    all_ac().wait_recv()
    gout[...] = ag2[...]

    def sent(s):
        for copy in halo_x(s) + halo_d(s):
            copy.wait_send()
        copy_c(s).wait_send()
        all_a(s).wait_send()

        @pl.when(x == s)
        def _():
            part = r2s.at[s, slice(1, nb)]
            remote(part, part, s_b.at[s], at_b(1, s)).wait_send()

        @pl.when(x != s)
        def _():
            remote(r2s.at[s], r2s.at[s], s_b.at[s], at_b(1, s)).wait_send()
            copy_f(s).wait_send()

        @pl.when(c == 0)
        def _():
            copy_h(s).wait_send()

        @pl.when(c == 1)
        def _():
            copy_g(s + 1).wait_send()

    each(0, blocks, sent)
    for d in range(1, nx):
        copy_w(d).wait_send()
    all_bg().wait_send()
    each(1, na, lambda d: copy_ag(d).wait_send())
    all_ac().wait_send()


def on_device(nx, ny, nz, pixels, video, cotangent, spatial_weights, temporal_weights):
    blocks = nx
    tile = (2, 2, C, C)
    rows = 6 * C
    rows1 = rows // ny
    rows2 = (rows1 // nz + 7) // 8 * 8
    vmem = pltpu.VMEM
    dma = pltpu.SemaphoreType.DMA
    scratch = [
        vmem((blocks, 4, 2, C, C), BF16),
        vmem((blocks,) + tile, F32),
        vmem((blocks,) + tile, BF16),
        vmem((blocks,) + tile, BF16),
        vmem((blocks + 1,) + tile, BF16),
        vmem((blocks + 1,) + tile, BF16),
        vmem((blocks, 4, 2, C, C), BF16),
        vmem((2, 2 * C, 3 * C), BF16),
        vmem((2, 2 * C, 3 * C), F32),
        vmem((2 * C, 2 * C), F32),
        vmem((blocks, 12, C, C), BF16),
        vmem((blocks, 3 * C, 3 * C), BF16),
        vmem((blocks, 3 * C, 3 * C), BF16),
        vmem((blocks, 2 * C, 2 * C), BF16),
        vmem((blocks, 2 * C, 2 * C), BF16),
        vmem((blocks, 2, rows, C), BF16),
        vmem((blocks, rows, C), BF16),
        vmem((blocks, ny, rows1, C), BF16),
        vmem((blocks, ny, rows1, C), BF16),
        vmem((rows1, C), F32),
        vmem((blocks, nz, rows2, C), F32),
        vmem((nx * nz, rows2, C), F32),
        vmem((nz, rows2, C), F32),
        vmem((2, ny, rows1, C), BF16),
        dma((5,)),
        dma((blocks, 2, 2)),
        dma((blocks, 2, 2)),
        dma((blocks, 2)),
        dma((blocks + 1, 2)),
        dma((nx, 2)),
        dma((nx, 2)),
        dma((blocks, 2)),
        dma((blocks, 2)),
        dma((blocks, 2)),
        dma((2,)),
        dma((ny, 2)),
        dma((2,)),
    ]
    grads, grad_video = pl.pallas_call(
        functools.partial(kernel, nx, ny, nz, 1.0 / float(pixels) ** 0.5),
        out_shape=(
            jax.ShapeDtypeStruct((2, ny, rows1, C), BF16),
            jax.ShapeDtypeStruct(tile, BF16),
        ),
        in_specs=[pl.BlockSpec(memory_space=pl.ANY)] * 4,
        out_specs=(pl.BlockSpec(memory_space=vmem),) * 2,
        scratch_shapes=scratch,
        compiler_params=pltpu.CompilerParams(
            collective_id=0, has_side_effects=True, vmem_limit_bytes=60 << 20
        ),
    )(video, cotangent, spatial_weights, temporal_weights)
    grads = grads.reshape(1, 12, C, C).astype(F32)
    return grads[:, :9], grads[:, 9:], grad_video


def solution(mesh):
    nx = mesh.shape["section"]
    space = mesh.shape["space"]
    nz = 1 << ((space.bit_length() - 1 + 1) // 2)
    ny = space // nz
    frames = 2 * mesh.shape["tm"]
    height = 2 * nx * space
    pixels = frames * height * C
    tiles = P("tm", ("section", "space"), None, None)
    owned = P("section", None, None, None)
    return jax.shard_map(
        functools.partial(on_device, nx, ny, nz, pixels),
        mesh=mesh,
        in_specs=(tiles, tiles, owned, owned),
        out_specs=(owned, owned, tiles),
        check_vma=False,
    )
```

```python
import functools

import jax
import jax.numpy as jnp
from jax import lax
from jax.experimental import pallas as pl
from jax.experimental.pallas import tpu as pltpu
from jax.sharding import PartitionSpec as P

MESH = pl.DeviceIdType.MESH
F32 = jnp.float32
BF16 = jnp.bfloat16
C = 128


def nn(a, b):
    return jnp.dot(a, b, preferred_element_type=F32)


def nt(a, b):
    return lax.dot_general(a, b, (((1,), (1,)), ((), ())), preferred_element_type=F32)


def tn(a, b):
    return lax.dot_general(a, b, (((0,), (0,)), ((), ())), preferred_element_type=F32)


def taken_back(v):
    return pltpu.roll(v, v.shape[0] - 1, 0)


def taken_on(v):
    return pltpu.roll(v, 1, 0)


def flat(v):
    return v.reshape(-1, v.shape[-1])


def side(*parts):
    return jnp.concatenate([flat(v) for v in parts], axis=1)


def kernel(
    nx, ny, nz, factor,
    video, cotangent, sw, tw,
    gout, gvid,
    vpad, gpad, mask, xs, dcoef, hs, hp, gs, gl, das, da3, gm, yacc, tacc, gsend, gback,
    wr, wk, wb, town, tprev,
    gb, rb, r1s, r1r, r2t, r2s, r3r, ag1, ag2,
    s_in, s_v, s_vs, s_q, s_qs, s_o, s_h, s_g, s_w, s_f, s_c, s_a, s_b, s_bg, s_ag, s_ac,
):
    blocks = nx
    x = lax.axis_index("section")
    c = lax.axis_index("tm")
    sp = lax.axis_index("space")
    y = sp // nz
    z = sp % nz
    other = 1 - c
    partner = (x, other, sp)
    na = r1s.shape[1]
    nb = r2s.shape[1]
    rows1 = r1s.shape[2]
    rows2 = rows1 // nb
    ia = y * (1 - c) + z * c
    ib = z * (1 - c) + y * c
    half = C // 2
    mine = pl.ds(pl.multiple_of(c * half, half), half)

    th = 2 * nz
    tw_ = C // nz
    rim = 2 * blocks
    side_rim = 8
    wh, ww = xs.shape[2], xs.shape[3]
    lines = nx * ny
    line = x * ny + y
    line_up = (line + lines - 1) % lines
    line_down = (line + 1) % lines
    own_rows = slice(rim, rim + th)

    def at_line(k, d):
        return (k // ny, c, (k % ny) * nz + (z + d) % nz)

    def at_x(d):
        return ((x + d) % nx, c, sp)

    def at_a(d):
        return (x, c, ((y + d * (1 - c)) % ny) * nz + (z + d * c) % nz)

    def at_b(d, owner):
        return (owner, c, ((y + d * c) % ny) * nz + (z + d * (1 - c)) % nz)

    def remote(src, dst, sems, device):
        return remote2(src, dst, sems.at[0], sems.at[1], device)

    def remote2(src, dst, send, recv, device):
        return pltpu.make_async_remote_copy(
            src_ref=src, dst_ref=dst, send_sem=send, recv_sem=recv,
            device_id=device, device_id_type=MESH,
        )

    def each(lo, hi, body):
        def step(i, carry):
            body(i)
            return carry
        lax.fori_loop(lo, hi, step, 0)

    def window(pad, dst, sends, recvs, k, row, d, group):
        to = (z + d) % nz
        cols = pl.ds(pl.multiple_of(to * tw_, tw_), ww)
        return remote2(
            pad.at[:, :, cols], dst.at[:, pl.ds(row, 2)],
            sends.at[group * nz + d], recvs.at[row // 2], at_line(k, d),
        )

    def windows(pad, dst, sends, recvs, reach, act):
        each(1, nz, lambda d: act(window(pad, dst, sends, recvs, line, rim + 2 * z, d, 0)))

        @pl.when(2 * z >= th - reach)
        def _():
            row = rim - th + 2 * z
            each(0, nz, lambda d: act(window(pad, dst, sends, recvs, line_down, row, d, 1)))

        @pl.when(2 * z < reach)
        def _():
            row = rim + th + 2 * z
            each(0, nz, lambda d: act(window(pad, dst, sends, recvs, line_up, row, d, 2)))

    def own_part(pad, dst, sem):
        cols = pl.ds(pl.multiple_of(z * tw_, tw_), ww)
        return pltpu.make_async_copy(
            pad.at[:, :, cols], dst.at[:, pl.ds(rim + 2 * z, 2)], sem
        )

    def wait_window(pad, dst, sends, recvs, reach):
        def one(pair):
            @pl.when(pair != rim // 2 + z)
            def _():
                remote2(
                    pad.at[:, :, pl.ds(0, ww)], dst.at[:, pl.ds(2 * pair, 2)],
                    sends.at[0], recvs.at[pair], partner,
                ).wait_recv()
        each((rim - reach) // 2, (rim + th + reach) // 2, one)

    def h_rows(s):
        return slice(s + 1, wh - s - 1) if s < blocks - 1 else own_rows

    def copy_h(s):
        rows = h_rows(s)
        return remote(hs.at[s, :, rows], hp.at[s, :, rows], s_h.at[s], partner)

    def copy_g(s):
        rows = slice(rim - s, rim + th + s)
        return remote(gs.at[s, :, rows], gl.at[s, :, rows], s_g.at[s], partner)

    def copy_o(d):
        cols = pl.ds(pl.multiple_of(z * tw_, tw_), tw_)
        return remote(gsend.at[(z + d) % nz], gback.at[:, :, cols], s_o, at_line(line, d))

    def copy_w(d):
        return remote(wr.at[x, :, mine], wr.at[x, :, mine], s_w.at[d], at_x(d))

    def copy_f(b):
        return remote(wr.at[b, :, mine], wr.at[b, :, mine], s_f.at[b], partner)

    def copy_c(s):
        return remote(gb.at[s, other], rb.at[s], s_c.at[s], partner)

    def copy_a(s, d):
        return remote(r1s.at[s, (ia + d) % na], r1r.at[s, d], s_a.at[s], at_a(d))

    def all_a(s):
        part = slice(1, na)
        return remote(r1s.at[s, part], r1r.at[s, part], s_a.at[s], at_a(1))

    def copy_b(s, d):
        slot = ((s + nx - x) % nx) * nb + d
        return remote(r2s.at[s, (ib + d) % nb], r3r.at[slot], s_b.at[s], at_b(d, s))

    def copy_bg(d):
        return remote(ag1.at[ib], ag1.at[ib], s_bg, at_b(d, x))

    def all_bg():
        part = ag1.at[slice(1, nb)]
        return remote(part, part, s_bg, at_b(1, x))

    def copy_ag(d):
        return remote(ag2.at[c, ia], ag2.at[c, ia], s_ag.at[d], at_a(d))

    def copy_ac(d):
        j = (ia + na - d) % na
        return remote(ag2.at[c, j], ag2.at[c, j], s_ac, partner)

    def all_ac():
        return remote(ag2.at[c], ag2.at[c], s_ac, partner)

    loads = [
        pltpu.make_async_copy(video, vpad.at[:, :, pl.ds(side_rim, C)], s_in.at[0]),
        pltpu.make_async_copy(sw.at[0], wr.at[x, pl.ds(0, 9)], s_in.at[1]),
        pltpu.make_async_copy(tw.at[0], wr.at[x, pl.ds(9, 3)], s_in.at[2]),
        pltpu.make_async_copy(cotangent, gpad.at[:, :, pl.ds(side_rim, C)], s_in.at[3]),
    ]
    for load in loads:
        load.start()

    barrier = pltpu.get_barrier_semaphore()
    peers = [partner]
    peers += [at_line(line_up, d) for d in range(nz)]
    peers += [at_line(line_down, d) for d in range(nz)]
    peers += [at_x(d) for d in range(1, nx)]
    peers += [at_a(d) for d in range(1, na)]
    peers += [at_b(d, (x + e) % nx) for e in range(nx) for d in range(1, nb)]
    for peer in peers:
        pl.semaphore_signal(barrier, inc=1, device_id=peer, device_id_type=MESH)

    for pad in (vpad, gpad):
        edge = jnp.zeros((2, 2, side_rim, C), BF16)
        pad[:, :, 0:side_rim] = edge
        pad[:, :, side_rim + C:] = edge

    for load in loads:
        load.wait()
    pl.semaphore_wait(barrier, len(peers))

    windows(vpad, xs.at[0], s_vs, s_v, rim, lambda copy: copy.start())
    own_part(vpad, xs.at[0], s_in.at[4]).start()
    for d in range(1, nx):
        copy_w(d).start()
    own_part(gpad, gs.at[blocks], s_in.at[5]).start()

    frame_row = line * th - rim + lax.broadcasted_iota(jnp.int32, mask.shape, 0)
    frame_col = z * tw_ - side_rim + lax.broadcasted_iota(jnp.int32, mask.shape, 1)
    inside = (frame_row >= 0) & (frame_row < lines * th) & (frame_col >= 0) & (frame_col < C)
    mask[...] = jnp.where(inside, 1.0, 0.0)

    @pl.when(c == 0)
    def _():
        hp[...] = jnp.zeros_like(hp)

    for b in range(blocks):
        @pl.when(x != b)
        def _():
            copy_w((x + nx - b) % nx).wait_recv()
            copy_f(b).start()

    def build(s):
        @pl.when(x != s)
        def _():
            copy_f(s).wait_recv()

        for ky in range(3):
            for kx in range(3):
                tap = wr[s, 3 * ky + kx]
                wk[s, ky * C:(ky + 1) * C, kx * C:(kx + 1) * C] = tap
                wb[s, kx * C:(kx + 1) * C, (2 - ky) * C:(3 - ky) * C] = tap
        zero = jnp.zeros((C, C), BF16)
        town[s, 0:C, 0:C] = wr[s, 11]
        town[s, 0:C, C:2 * C] = wr[s, 10]
        town[s, C:2 * C, 0:C] = zero
        town[s, C:2 * C, C:2 * C] = wr[s, 11]
        tprev[s, 0:C, 0:C] = wr[s, 9]
        tprev[s, 0:C, C:2 * C] = zero
        tprev[s, C:2 * C, 0:C] = wr[s, 10]
        tprev[s, C:2 * C, C:2 * C] = wr[s, 9]

    each(0, blocks, build)

    wait_window(vpad, xs.at[0], s_vs, s_v, rim)
    own_part(vpad, xs.at[0], s_in.at[4]).wait()
    windows(gpad, gs.at[blocks], s_qs, s_q, blocks, lambda copy: copy.start())

    @pl.when(line == 0)
    def _():
        xs[0, :, 0:rim] = jnp.zeros((2, rim, ww, C), BF16)

    @pl.when(line == lines - 1)
    def _():
        xs[0, :, rim + th:] = jnp.zeros((2, rim, ww, C), BF16)

    two = 2 * ww

    def forward(s):
        lo, hi = s + 1, wh - s - 1
        n = hi - lo
        for f in range(2):
            around = side(xs[s, f, lo - 1:hi - 1], xs[s, f, lo:hi], xs[s, f, lo + 1:hi + 1])
            yacc[f, 0:n * ww] = nn(around, wk[s])

        def activate(i):
            rows = pl.ds(lo + 2 * i, 2)
            for f in range(2):
                part = yacc[f, pl.ds(pl.multiple_of(i * two, two), two)]
                pre = taken_on(part[:, 0:C]) + part[:, C:2 * C] + taken_back(part[:, 2 * C:])
                sig = 0.5 * jnp.tanh(0.5 * pre) + 0.5
                hs[s, f, rows] = (pre * sig).astype(BF16).reshape(2, ww, C)
                dcoef[s, f, rows] = (sig * (1.0 + pre * (1.0 - sig))).reshape(2, ww, C)

        each(0, n // 2, activate)

        @pl.when(c == 0)
        def _():
            copy_h(s).start()

        if s == blocks - 1:
            @pl.when(c == 1)
            def _():
                copy_h(s).wait_recv()
            return

        tacc[0:n * ww] = nn(side(hs[s, 0, lo:hi], hs[s, 1, lo:hi]), town[s])

        @pl.when(c == 1)
        def _():
            copy_h(s).wait_recv()
            tacc[0:n * ww] += nn(side(hp[s, 0, lo:hi], hp[s, 1, lo:hi]), tprev[s])

        def add(i):
            rows = pl.ds(lo + 2 * i, 2)
            for f in range(2):
                mix = tacc[pl.ds(pl.multiple_of(i * two, two), two), f * C:(f + 1) * C]
                held = xs[s, f, rows].astype(F32) + mix.reshape(2, ww, C)
                xs[s + 1, f, rows] = (held * mask[rows]).astype(BF16)

        each(0, n // 2, add)

    for s in range(blocks):
        forward(s)

    wait_window(gpad, gs.at[blocks], s_qs, s_q, blocks)
    own_part(gpad, gs.at[blocks], s_in.at[5]).wait()

    @pl.when(line == 0)
    def _():
        gs[blocks, :, rim - blocks:rim] = jnp.zeros((2, blocks, ww, C), BF16)

    @pl.when(line == lines - 1)
    def _():
        gs[blocks, :, rim + th:rim + th + blocks] = jnp.zeros((2, blocks, ww, C), BF16)

    @pl.when(c == 1)
    def _():
        copy_g(blocks).start()

    def core_sum(s):
        copy_c(s).wait_recv()
        for j in range(na):
            rows = slice(j * rows1, (j + 1) * rows1)
            r1s[s, j] = (gb[s, c, rows].astype(F32) + rb[s, rows].astype(F32)).astype(BF16)
        each(1, na, lambda d: copy_a(s, d).start())

    def a_sum(s):
        all_a(s).wait_recv()
        part = r1s[s, ia].astype(F32)
        for d in range(1, na):
            part = part + r1r[s, d].astype(F32)
        r2t[...] = part
        for j in range(nb):
            r2s[s, j, 0:rows2] = r2t[j * rows2:(j + 1) * rows2]

        @pl.when(x == s)
        def _():
            r3r[0] = r2s[s, ib]

        @pl.when(x != s)
        def _():
            copy_b(s, 0).start()

        each(1, nb, lambda d: copy_b(s, d).start())

    column = lax.broadcasted_iota(jnp.int32, (2, ww, C), 1)
    own_column = (column >= side_rim) & (column < side_rim + tw_)

    def weight_grads(s):
        def prepare(i):
            rows = pl.ds(rim + 2 * i, 2)
            px = pl.ds(pl.multiple_of(i * two, two), two)
            for f in range(2):
                da = flat(jnp.where(own_column, das[f, rows].astype(F32), 0.0))
                da3[f, px, 0:C] = taken_back(da).astype(BF16)
                da3[f, px, C:2 * C] = da.astype(BF16)
                da3[f, px, 2 * C:3 * C] = taken_on(da).astype(BF16)
                grad = jnp.where(own_column, gs[s + 1, f, rows].astype(F32), 0.0)
                gm[px, f * C:(f + 1) * C] = flat(grad).astype(BF16)

        each(0, th // 2, prepare)
        outer = tn(
            side(hp[s, 0, own_rows], hp[s, 1, own_rows], hs[s, 0, own_rows], hs[s, 1, own_rows]),
            gm[...],
        )
        for kt in range(3):
            gt = outer[kt * C:(kt + 1) * C, 0:C] + outer[(kt + 1) * C:(kt + 2) * C, C:2 * C]
            gb[s, 1, (3 + kt) * C:(4 + kt) * C] = gt.astype(BF16)
        for ky in range(3):
            rows = slice(rim + ky - 1, rim + ky - 1 + th)
            gw = tn(flat(xs[s, 0, rows]), da3[0]) + tn(flat(xs[s, 1, rows]), da3[1])
            for kx in range(3):
                tap = 3 * ky + kx
                row = (tap % 6) * C
                gb[s, tap // 6, row:row + C] = gw[:, kx * C:(kx + 1) * C].astype(BF16)
        copy_c(s).start()

    def back_rows(s):
        lo, hi = rim - s, rim + th + s
        n = hi - lo
        for f in range(2):
            around = side(das[f, lo - 1:hi - 1], das[f, lo:hi], das[f, lo + 1:hi + 1])
            yacc[f, 0:n * ww] = nt(around, wb[s])

        def add(i):
            rows = pl.ds(lo + 2 * i, 2)
            for f in range(2):
                part = yacc[f, pl.ds(pl.multiple_of(i * two, two), two)]
                back = taken_back(part[:, 0:C]) + part[:, C:2 * C] + taken_on(part[:, 2 * C:])
                grad = gs[s + 1, f, rows].astype(F32) + back.reshape(2, ww, C)
                if s > 0:
                    gs[s, f, rows] = grad.astype(BF16)
                else:
                    gsend[i, f] = grad[:, side_rim:side_rim + tw_].astype(BF16)

        each(0, n // 2, add)

    def backward(s):
        lo, hi = rim - s - 1, rim + th + s + 1
        n = hi - lo
        tacc[0:n * ww] = nt(side(gs[s + 1, 0, lo:hi], gs[s + 1, 1, lo:hi]), town[s])

        @pl.when(c == 0)
        def _():
            copy_g(s + 1).wait_recv()
            tacc[0:n * ww] += nt(side(gl[s + 1, 0, lo:hi], gl[s + 1, 1, lo:hi]), tprev[s])

        def activate(i):
            rows = pl.ds(lo + 2 * i, 2)
            for f in range(2):
                dh = tacc[pl.ds(pl.multiple_of(i * two, two), two), f * C:(f + 1) * C]
                da = dh.reshape(2, ww, C) * dcoef[s, f, rows] * mask[rows]
                das[f, rows] = da.astype(BF16)

        each(0, n // 2, activate)

        if s == 0:
            weight_grads(0)
        back_rows(s)
        if s > 0:
            @pl.when(c == 1)
            def _():
                copy_g(s).start()

            weight_grads(s)
        else:
            each(1, nz, lambda d: copy_o(d).start())
            own_cols = pl.ds(pl.multiple_of(z * tw_, tw_), tw_)
            gback[:, :, own_cols] = gsend[z]
        if s < blocks - 1:
            a_sum(s + 1)
        core_sum(s)

    for s in reversed(range(blocks)):
        backward(s)

    a_sum(0)
    sent_o = gsend.at[slice(1, nz)]
    remote(sent_o, sent_o, s_o, partner).wait_recv()
    gvid[...] = gback[...]

    others = slice(1, nx * nb)
    remote(r3r.at[others], r3r.at[others], s_b.at[x], at_b(1, x)).wait_recv()
    part = r3r[0]
    for d in range(1, nx * nb):
        part = part + r3r[d]
    ag1[ib] = part * factor
    each(1, nb, lambda d: copy_bg(d).start())
    all_bg().wait_recv()
    for j in range(nb):
        r2t[j * rows2:(j + 1) * rows2] = ag1[j, 0:rows2]
    ag2[c, ia] = r2t[...].astype(BF16)
    each(1, na, lambda d: copy_ag(d).start())
    copy_ac(0).start()

    def hand_on(d):
        copy_ag(d).wait_recv()
        copy_ac(d).start()

    each(1, na, hand_on)
    all_ac().wait_recv()
    gout[...] = ag2[...]

    windows(vpad, xs.at[0], s_vs, s_v, rim, lambda copy: copy.wait_send())
    windows(gpad, gs.at[blocks], s_qs, s_q, blocks, lambda copy: copy.wait_send())
    remote(sent_o, sent_o, s_o, partner).wait_send()
    for s in range(blocks):
        copy_c(s).wait_send()
        all_a(s).wait_send()

        @pl.when(x == s)
        def _():
            part = r2s.at[s, slice(1, nb)]
            remote(part, part, s_b.at[s], at_b(1, s)).wait_send()

        @pl.when(x != s)
        def _():
            remote(r2s.at[s], r2s.at[s], s_b.at[s], at_b(1, s)).wait_send()
            copy_f(s).wait_send()

        @pl.when(c == 0)
        def _():
            copy_h(s).wait_send()

        @pl.when(c == 1)
        def _():
            copy_g(s + 1).wait_send()

    for d in range(1, nx):
        copy_w(d).wait_send()
    all_bg().wait_send()
    each(1, na, lambda d: copy_ag(d).wait_send())
    all_ac().wait_send()


def on_device(nx, ny, nz, pixels, video, cotangent, spatial_weights, temporal_weights):
    blocks = nx
    tile = (2, 2, C, C)
    rows = 6 * C
    rows1 = rows // ny
    rows2 = (rows1 // nz + 7) // 8 * 8
    vmem = pltpu.VMEM
    dma = pltpu.SemaphoreType.DMA
    wh, ww = 2 * nz + 4 * blocks, C // nz + 16
    win = (2, wh, ww, C)
    scratch = [
        vmem((2, 2, C + 16, C), BF16),
        vmem((2, 2, C + 16, C), BF16),
        vmem((wh, ww, C), F32),
        vmem((blocks,) + win, BF16),
        vmem((blocks,) + win, F32),
        vmem((blocks,) + win, BF16),
        vmem((blocks,) + win, BF16),
        vmem((blocks + 1,) + win, BF16),
        vmem((blocks + 1,) + win, BF16),
        vmem(win, BF16),
        vmem((2, 2 * nz * ww, 3 * C), BF16),
        vmem((2 * nz * ww, 2 * C), BF16),
        vmem((2, wh * ww, 3 * C), F32),
        vmem((wh * ww, 2 * C), F32),
        vmem((nz, 2, 2, C // nz, C), BF16),
        vmem(tile, BF16),
        vmem((blocks, 12, C, C), BF16),
        vmem((blocks, 3 * C, 3 * C), BF16),
        vmem((blocks, 3 * C, 3 * C), BF16),
        vmem((blocks, 2 * C, 2 * C), BF16),
        vmem((blocks, 2 * C, 2 * C), BF16),
        vmem((blocks, 2, rows, C), BF16),
        vmem((blocks, rows, C), BF16),
        vmem((blocks, ny, rows1, C), BF16),
        vmem((blocks, ny, rows1, C), BF16),
        vmem((rows1, C), F32),
        vmem((blocks, nz, rows2, C), F32),
        vmem((nx * nz, rows2, C), F32),
        vmem((nz, rows2, C), F32),
        vmem((2, ny, rows1, C), BF16),
        dma((6,)),
        dma((wh // 2,)),
        dma((3 * nz,)),
        dma((wh // 2,)),
        dma((3 * nz,)),
        dma((2,)),
        dma((blocks, 2)),
        dma((blocks + 1, 2)),
        dma((nx, 2)),
        dma((nx, 2)),
        dma((blocks, 2)),
        dma((blocks, 2)),
        dma((blocks, 2)),
        dma((2,)),
        dma((ny, 2)),
        dma((2,)),
    ]
    grads, grad_video = pl.pallas_call(
        functools.partial(kernel, nx, ny, nz, 1.0 / float(pixels) ** 0.5),
        out_shape=(
            jax.ShapeDtypeStruct((2, ny, rows1, C), BF16),
            jax.ShapeDtypeStruct(tile, BF16),
        ),
        in_specs=[pl.BlockSpec(memory_space=pl.ANY)] * 4,
        out_specs=(pl.BlockSpec(memory_space=vmem),) * 2,
        scratch_shapes=scratch,
        compiler_params=pltpu.CompilerParams(
            collective_id=0, has_side_effects=True, vmem_limit_bytes=60 << 20
        ),
    )(video, cotangent, spatial_weights, temporal_weights)
    grads = grads.reshape(1, 12, C, C).astype(F32)
    return grads[:, :9], grads[:, 9:], grad_video


def solution(mesh):
    nx = mesh.shape["section"]
    space = mesh.shape["space"]
    nz = 1 << ((space.bit_length() - 1 + 1) // 2)
    ny = space // nz
    frames = 2 * mesh.shape["tm"]
    height = 2 * nx * space
    pixels = frames * height * C
    tiles = P("tm", ("section", "space"), None, None)
    owned = P("section", None, None, None)
    return jax.shard_map(
        functools.partial(on_device, nx, ny, nz, pixels),
        mesh=mesh,
        in_specs=(tiles, tiles, owned, owned),
        out_specs=(owned, owned, tiles),
        check_vma=False,
    )
```

```python
import functools

import jax
import jax.numpy as jnp
from jax import lax
from jax.experimental import pallas as pl
from jax.experimental.pallas import tpu as pltpu
from jax.sharding import PartitionSpec as P

MESH = pl.DeviceIdType.MESH
F32 = jnp.float32
BF16 = jnp.bfloat16
C = 128


def nn(a, b):
    return jnp.dot(a, b, preferred_element_type=F32)


def nt(a, b):
    return lax.dot_general(a, b, (((1,), (1,)), ((), ())), preferred_element_type=F32)


def tn(a, b):
    return lax.dot_general(a, b, (((0,), (0,)), ((), ())), preferred_element_type=F32)


def taken_back(v):
    return pltpu.roll(v, v.shape[0] - 1, 0)


def taken_on(v):
    return pltpu.roll(v, 1, 0)


def flat(v):
    return v.reshape(-1, v.shape[-1])


def side(*parts):
    return jnp.concatenate([flat(v) for v in parts], axis=1)


def kernel(
    nx, ny, nz, factor,
    video, cotangent, sw, tw,
    gout, gvid,
    vpad, gpad, mask, xs, dcoef, hs, hp, gs, gl, das, da3, gm, yacc, tacc, gsend, gback,
    wr, wk, wb, town, tprev,
    gb, rb, r1s, r1r, r2t, r2s, r3r, ag1, ag2,
    s_in, s_v, s_vs, s_q, s_qs, s_o, s_h, s_g, s_w, s_f, s_c, s_a, s_b, s_bg, s_ag, s_ac,
):
    blocks = nx
    x = lax.axis_index("section")
    c = lax.axis_index("tm")
    sp = lax.axis_index("space")
    y = sp // nz
    z = sp % nz
    other = 1 - c
    partner = (x, other, sp)
    na = r1s.shape[1]
    nb = r2s.shape[1]
    rows1 = r1s.shape[2]
    rows2 = rows1 // nb
    ia = y * (1 - c) + z * c
    ib = z * (1 - c) + y * c
    half = C // 2
    mine = pl.ds(pl.multiple_of(c * half, half), half)

    th = 2 * nz
    tw_ = C // nz
    rim = 2 * blocks
    side_rim = 8
    wh, ww = xs.shape[2], xs.shape[3]
    lines = nx * ny
    line = x * ny + y
    line_up = (line + lines - 1) % lines
    line_down = (line + 1) % lines
    own_rows = slice(rim, rim + th)

    def at_line(k, d):
        return (k // ny, c, (k % ny) * nz + (z + d) % nz)

    def at_x(d):
        return ((x + d) % nx, c, sp)

    def at_a(d):
        return (x, c, ((y + d * (1 - c)) % ny) * nz + (z + d * c) % nz)

    def at_b(d, owner):
        return (owner, c, ((y + d * c) % ny) * nz + (z + d * (1 - c)) % nz)

    def remote(src, dst, sems, device):
        return remote2(src, dst, sems.at[0], sems.at[1], device)

    def remote2(src, dst, send, recv, device):
        return pltpu.make_async_remote_copy(
            src_ref=src, dst_ref=dst, send_sem=send, recv_sem=recv,
            device_id=device, device_id_type=MESH,
        )

    def each(lo, hi, body):
        def step(i, carry):
            body(i)
            return carry
        lax.fori_loop(lo, hi, step, 0)

    def window(pad, dst, sends, recvs, k, row, d, group):
        to = (z + d) % nz
        cols = pl.ds(pl.multiple_of(to * tw_, tw_), ww)
        return remote2(
            pad.at[:, :, cols], dst.at[:, pl.ds(row, 2)],
            sends.at[group * nz + d], recvs.at[row // 2], at_line(k, d),
        )

    def windows(pad, dst, sends, recvs, reach, act):
        each(1, nz, lambda d: act(window(pad, dst, sends, recvs, line, rim + 2 * z, d, 0)))

        @pl.when(2 * z >= th - reach)
        def _():
            row = rim - th + 2 * z
            each(0, nz, lambda d: act(window(pad, dst, sends, recvs, line_down, row, d, 1)))

        @pl.when(2 * z < reach)
        def _():
            row = rim + th + 2 * z
            each(0, nz, lambda d: act(window(pad, dst, sends, recvs, line_up, row, d, 2)))

    def own_part(pad, dst, sem):
        cols = pl.ds(pl.multiple_of(z * tw_, tw_), ww)
        return pltpu.make_async_copy(
            pad.at[:, :, cols], dst.at[:, pl.ds(rim + 2 * z, 2)], sem
        )

    def wait_window(pad, dst, sends, recvs, reach):
        def one(pair):
            @pl.when(pair != rim // 2 + z)
            def _():
                remote2(
                    pad.at[:, :, pl.ds(0, ww)], dst.at[:, pl.ds(2 * pair, 2)],
                    sends.at[0], recvs.at[pair], partner,
                ).wait_recv()
        each((rim - reach) // 2, (rim + th + reach) // 2, one)

    def h_rows(s):
        return slice(s + 1, wh - s - 1) if s < blocks - 1 else own_rows

    def copy_h(s):
        rows = h_rows(s)
        return remote(hs.at[s, :, rows], hp.at[s, :, rows], s_h.at[s], partner)

    def copy_g(s):
        rows = slice(rim - s, rim + th + s)
        return remote(gs.at[s, :, rows], gl.at[s, :, rows], s_g.at[s], partner)

    def copy_o(d):
        cols = pl.ds(pl.multiple_of(z * tw_, tw_), tw_)
        return remote(gsend.at[(z + d) % nz], gback.at[:, :, cols], s_o, at_line(line, d))

    def copy_w(d):
        return remote(wr.at[x, :, mine], wr.at[x, :, mine], s_w.at[d], at_x(d))

    def copy_f(b):
        return remote(wr.at[b, :, mine], wr.at[b, :, mine], s_f.at[b], partner)

    def copy_c(s):
        return remote(gb.at[s, other], rb.at[s], s_c.at[s], partner)

    def copy_a(s, d):
        return remote(r1s.at[s, (ia + d) % na], r1r.at[s, d], s_a.at[s], at_a(d))

    def all_a(s):
        part = slice(1, na)
        return remote(r1s.at[s, part], r1r.at[s, part], s_a.at[s], at_a(1))

    def copy_b(s, d):
        slot = ((s + nx - x) % nx) * nb + d
        return remote(r2s.at[s, (ib + d) % nb], r3r.at[slot], s_b.at[s], at_b(d, s))

    def copy_bg(d):
        return remote(ag1.at[ib], ag1.at[ib], s_bg, at_b(d, x))

    def all_bg():
        part = ag1.at[slice(1, nb)]
        return remote(part, part, s_bg, at_b(1, x))

    def copy_ag(d):
        return remote(ag2.at[c, ia], ag2.at[c, ia], s_ag.at[d], at_a(d))

    def copy_ac(d):
        j = (ia + na - d) % na
        return remote(ag2.at[c, j], ag2.at[c, j], s_ac, partner)

    def all_ac():
        return remote(ag2.at[c], ag2.at[c], s_ac, partner)

    loads = [
        pltpu.make_async_copy(video, vpad.at[:, :, pl.ds(side_rim, C)], s_in.at[0]),
        pltpu.make_async_copy(sw.at[0], wr.at[x, pl.ds(0, 9)], s_in.at[1]),
        pltpu.make_async_copy(tw.at[0], wr.at[x, pl.ds(9, 3)], s_in.at[2]),
        pltpu.make_async_copy(cotangent, gpad.at[:, :, pl.ds(side_rim, C)], s_in.at[3]),
    ]
    for load in loads:
        load.start()

    barrier = pltpu.get_barrier_semaphore()
    peers = [partner]
    peers += [at_line(line_up, d) for d in range(nz)]
    peers += [at_line(line_down, d) for d in range(nz)]
    peers += [at_x(d) for d in range(1, nx)]
    peers += [at_a(d) for d in range(1, na)]
    peers += [at_b(d, (x + e) % nx) for e in range(nx) for d in range(1, nb)]
    for peer in peers:
        pl.semaphore_signal(barrier, inc=1, device_id=peer, device_id_type=MESH)

    for pad in (vpad, gpad):
        edge = jnp.zeros((2, 2, side_rim, C), BF16)
        pad[:, :, 0:side_rim] = edge
        pad[:, :, side_rim + C:] = edge

    for load in loads:
        load.wait()
    pl.semaphore_wait(barrier, len(peers))

    windows(vpad, xs.at[0], s_vs, s_v, rim, lambda copy: copy.start())
    own_part(vpad, xs.at[0], s_in.at[4]).start()
    for d in range(1, nx):
        copy_w(d).start()
    own_part(gpad, gs.at[blocks], s_in.at[5]).start()

    frame_row = line * th - rim + lax.broadcasted_iota(jnp.int32, mask.shape, 0)
    frame_col = z * tw_ - side_rim + lax.broadcasted_iota(jnp.int32, mask.shape, 1)
    inside = (frame_row >= 0) & (frame_row < lines * th) & (frame_col >= 0) & (frame_col < C)
    mask[...] = jnp.where(inside, 1.0, 0.0)

    @pl.when(c == 0)
    def _():
        hp[...] = jnp.zeros_like(hp)

    for b in range(blocks):
        @pl.when(x != b)
        def _():
            copy_w((x + nx - b) % nx).wait_recv()
            copy_f(b).start()

    def build(s):
        @pl.when(x != s)
        def _():
            copy_f(s).wait_recv()

        for ky in range(3):
            for kx in range(3):
                tap = wr[s, 3 * ky + kx]
                wk[s, ky * C:(ky + 1) * C, kx * C:(kx + 1) * C] = tap
                wb[s, kx * C:(kx + 1) * C, (2 - ky) * C:(3 - ky) * C] = tap
        zero = jnp.zeros((C, C), BF16)
        town[s, 0:C, 0:C] = wr[s, 11]
        town[s, 0:C, C:2 * C] = wr[s, 10]
        town[s, C:2 * C, 0:C] = zero
        town[s, C:2 * C, C:2 * C] = wr[s, 11]
        tprev[s, 0:C, 0:C] = wr[s, 9]
        tprev[s, 0:C, C:2 * C] = zero
        tprev[s, C:2 * C, 0:C] = wr[s, 10]
        tprev[s, C:2 * C, C:2 * C] = wr[s, 9]

    each(0, blocks, build)

    wait_window(vpad, xs.at[0], s_vs, s_v, rim)
    own_part(vpad, xs.at[0], s_in.at[4]).wait()
    windows(gpad, gs.at[blocks], s_qs, s_q, blocks, lambda copy: copy.start())

    @pl.when(line == 0)
    def _():
        xs[0, :, 0:rim] = jnp.zeros((2, rim, ww, C), BF16)

    @pl.when(line == lines - 1)
    def _():
        xs[0, :, rim + th:] = jnp.zeros((2, rim, ww, C), BF16)

    two = 2 * ww

    def forward(s):
        lo, hi = s + 1, wh - s - 1
        n = hi - lo
        for f in range(2):
            around = side(xs[s, f, lo - 1:hi - 1], xs[s, f, lo:hi], xs[s, f, lo + 1:hi + 1])
            yacc[f, 0:n * ww] = nn(around, wk[s])

        def activate(i):
            rows = pl.ds(lo + 2 * i, 2)
            for f in range(2):
                part = yacc[f, pl.ds(pl.multiple_of(i * two, two), two)]
                pre = taken_on(part[:, 0:C]) + part[:, C:2 * C] + taken_back(part[:, 2 * C:])
                sig = 0.5 * jnp.tanh(0.5 * pre) + 0.5
                hs[s, f, rows] = (pre * sig).astype(BF16).reshape(2, ww, C)
                dcoef[s, f, rows] = (sig * (1.0 + pre * (1.0 - sig))).reshape(2, ww, C)

        each(0, n // 2, activate)

        @pl.when(c == 0)
        def _():
            copy_h(s).start()

        if s == blocks - 1:
            @pl.when(c == 1)
            def _():
                copy_h(s).wait_recv()
            return

        tacc[0:n * ww] = nn(side(hs[s, 0, lo:hi], hs[s, 1, lo:hi]), town[s])

        @pl.when(c == 1)
        def _():
            copy_h(s).wait_recv()
            tacc[0:n * ww] += nn(side(hp[s, 0, lo:hi], hp[s, 1, lo:hi]), tprev[s])

        def add(i):
            rows = pl.ds(lo + 2 * i, 2)
            for f in range(2):
                mix = tacc[pl.ds(pl.multiple_of(i * two, two), two), f * C:(f + 1) * C]
                held = xs[s, f, rows].astype(F32) + mix.reshape(2, ww, C)
                xs[s + 1, f, rows] = (held * mask[rows]).astype(BF16)

        each(0, n // 2, add)

    for s in range(blocks):
        forward(s)

    wait_window(gpad, gs.at[blocks], s_qs, s_q, blocks)
    own_part(gpad, gs.at[blocks], s_in.at[5]).wait()

    @pl.when(line == 0)
    def _():
        gs[blocks, :, rim - blocks:rim] = jnp.zeros((2, blocks, ww, C), BF16)

    @pl.when(line == lines - 1)
    def _():
        gs[blocks, :, rim + th:rim + th + blocks] = jnp.zeros((2, blocks, ww, C), BF16)

    @pl.when(c == 1)
    def _():
        copy_g(blocks).start()

    def core_sum(s):
        copy_c(s).wait_recv()
        for j in range(na):
            rows = slice(j * rows1, (j + 1) * rows1)
            r1s[s, j] = (gb[s, c, rows].astype(F32) + rb[s, rows].astype(F32)).astype(BF16)
        each(1, na, lambda d: copy_a(s, d).start())

    def a_sum(s):
        all_a(s).wait_recv()
        part = r1s[s, ia].astype(F32)
        for d in range(1, na):
            part = part + r1r[s, d].astype(F32)
        r2t[...] = part
        for j in range(nb):
            r2s[s, j, 0:rows2] = r2t[j * rows2:(j + 1) * rows2]

        @pl.when(x == s)
        def _():
            r3r[0] = r2s[s, ib]

        @pl.when(x != s)
        def _():
            copy_b(s, 0).start()

        each(1, nb, lambda d: copy_b(s, d).start())

    column = lax.broadcasted_iota(jnp.int32, (2, ww, C), 1)
    own_column = (column >= side_rim) & (column < side_rim + tw_)

    def weight_grads(s):
        def prepare(i):
            rows = pl.ds(rim + 2 * i, 2)
            px = pl.ds(pl.multiple_of(i * two, two), two)
            for f in range(2):
                da = flat(jnp.where(own_column, das[f, rows].astype(F32), 0.0))
                da3[f, px, 0:C] = taken_back(da).astype(BF16)
                da3[f, px, C:2 * C] = da.astype(BF16)
                da3[f, px, 2 * C:3 * C] = taken_on(da).astype(BF16)
                grad = jnp.where(own_column, gs[s + 1, f, rows].astype(F32), 0.0)
                gm[px, f * C:(f + 1) * C] = flat(grad).astype(BF16)

        each(0, th // 2, prepare)
        outer = tn(
            side(hp[s, 0, own_rows], hp[s, 1, own_rows], hs[s, 0, own_rows], hs[s, 1, own_rows]),
            gm[...],
        )
        for kt in range(3):
            gt = outer[kt * C:(kt + 1) * C, 0:C] + outer[(kt + 1) * C:(kt + 2) * C, C:2 * C]
            gb[s, 1, (3 + kt) * C:(4 + kt) * C] = gt.astype(BF16)
        for ky in range(3):
            rows = slice(rim + ky - 1, rim + ky - 1 + th)
            gw = tn(flat(xs[s, 0, rows]), da3[0]) + tn(flat(xs[s, 1, rows]), da3[1])
            for kx in range(3):
                tap = 3 * ky + kx
                row = (tap % 6) * C
                gb[s, tap // 6, row:row + C] = gw[:, kx * C:(kx + 1) * C].astype(BF16)
        copy_c(s).start()

    def back_rows(s):
        lo, hi = rim - s, rim + th + s
        n = hi - lo
        for f in range(2):
            around = side(das[f, lo - 1:hi - 1], das[f, lo:hi], das[f, lo + 1:hi + 1])
            yacc[f, 0:n * ww] = nt(around, wb[s])

        def add(i):
            rows = pl.ds(lo + 2 * i, 2)
            for f in range(2):
                part = yacc[f, pl.ds(pl.multiple_of(i * two, two), two)]
                back = taken_back(part[:, 0:C]) + part[:, C:2 * C] + taken_on(part[:, 2 * C:])
                grad = gs[s + 1, f, rows].astype(F32) + back.reshape(2, ww, C)
                if s > 0:
                    gs[s, f, rows] = grad.astype(BF16)
                else:
                    gsend[i, f] = grad[:, side_rim:side_rim + tw_].astype(BF16)

        each(0, n // 2, add)

    def backward(s):
        lo, hi = rim - s - 1, rim + th + s + 1
        n = hi - lo
        tacc[0:n * ww] = nt(side(gs[s + 1, 0, lo:hi], gs[s + 1, 1, lo:hi]), town[s])

        @pl.when(c == 0)
        def _():
            copy_g(s + 1).wait_recv()
            tacc[0:n * ww] += nt(side(gl[s + 1, 0, lo:hi], gl[s + 1, 1, lo:hi]), tprev[s])

        def activate(i):
            rows = pl.ds(lo + 2 * i, 2)
            for f in range(2):
                dh = tacc[pl.ds(pl.multiple_of(i * two, two), two), f * C:(f + 1) * C]
                da = dh.reshape(2, ww, C) * dcoef[s, f, rows] * mask[rows]
                das[f, rows] = da.astype(BF16)

        each(0, n // 2, activate)

        if s < blocks - 1:
            core_sum(s + 1)
        if s == 0:
            weight_grads(0)
        back_rows(s)
        if s > 0:
            @pl.when(c == 1)
            def _():
                copy_g(s).start()

            weight_grads(s)
        else:
            each(1, nz, lambda d: copy_o(d).start())
            own_cols = pl.ds(pl.multiple_of(z * tw_, tw_), tw_)
            gback[:, :, own_cols] = gsend[z]

    for s in reversed(range(blocks)):
        backward(s)

    core_sum(0)
    for s in reversed(range(blocks)):
        a_sum(s)
    sent_o = gsend.at[slice(1, nz)]
    remote(sent_o, sent_o, s_o, partner).wait_recv()
    gvid[...] = gback[...]

    others = slice(1, nx * nb)
    remote(r3r.at[others], r3r.at[others], s_b.at[x], at_b(1, x)).wait_recv()
    part = r3r[0]
    for d in range(1, nx * nb):
        part = part + r3r[d]
    ag1[ib] = part * factor
    each(1, nb, lambda d: copy_bg(d).start())
    all_bg().wait_recv()
    for j in range(nb):
        r2t[j * rows2:(j + 1) * rows2] = ag1[j, 0:rows2]
    ag2[c, ia] = r2t[...].astype(BF16)
    each(1, na, lambda d: copy_ag(d).start())
    copy_ac(0).start()

    def hand_on(d):
        copy_ag(d).wait_recv()
        copy_ac(d).start()

    each(1, na, hand_on)
    all_ac().wait_recv()
    gout[...] = ag2[...]

    windows(vpad, xs.at[0], s_vs, s_v, rim, lambda copy: copy.wait_send())
    windows(gpad, gs.at[blocks], s_qs, s_q, blocks, lambda copy: copy.wait_send())
    remote(sent_o, sent_o, s_o, partner).wait_send()
    for s in range(blocks):
        copy_c(s).wait_send()
        all_a(s).wait_send()

        @pl.when(x == s)
        def _():
            part = r2s.at[s, slice(1, nb)]
            remote(part, part, s_b.at[s], at_b(1, s)).wait_send()

        @pl.when(x != s)
        def _():
            remote(r2s.at[s], r2s.at[s], s_b.at[s], at_b(1, s)).wait_send()
            copy_f(s).wait_send()

        @pl.when(c == 0)
        def _():
            copy_h(s).wait_send()

        @pl.when(c == 1)
        def _():
            copy_g(s + 1).wait_send()

    for d in range(1, nx):
        copy_w(d).wait_send()
    all_bg().wait_send()
    each(1, na, lambda d: copy_ag(d).wait_send())
    all_ac().wait_send()


def on_device(nx, ny, nz, pixels, video, cotangent, spatial_weights, temporal_weights):
    blocks = nx
    tile = (2, 2, C, C)
    rows = 6 * C
    rows1 = rows // ny
    rows2 = (rows1 // nz + 7) // 8 * 8
    vmem = pltpu.VMEM
    dma = pltpu.SemaphoreType.DMA
    wh, ww = 2 * nz + 4 * blocks, C // nz + 16
    win = (2, wh, ww, C)
    scratch = [
        vmem((2, 2, C + 16, C), BF16),
        vmem((2, 2, C + 16, C), BF16),
        vmem((wh, ww, C), F32),
        vmem((blocks,) + win, BF16),
        vmem((blocks,) + win, F32),
        vmem((blocks,) + win, BF16),
        vmem((blocks,) + win, BF16),
        vmem((blocks + 1,) + win, BF16),
        vmem((blocks + 1,) + win, BF16),
        vmem(win, BF16),
        vmem((2, 2 * nz * ww, 3 * C), BF16),
        vmem((2 * nz * ww, 2 * C), BF16),
        vmem((2, wh * ww, 3 * C), F32),
        vmem((wh * ww, 2 * C), F32),
        vmem((nz, 2, 2, C // nz, C), BF16),
        vmem(tile, BF16),
        vmem((blocks, 12, C, C), BF16),
        vmem((blocks, 3 * C, 3 * C), BF16),
        vmem((blocks, 3 * C, 3 * C), BF16),
        vmem((blocks, 2 * C, 2 * C), BF16),
        vmem((blocks, 2 * C, 2 * C), BF16),
        vmem((blocks, 2, rows, C), BF16),
        vmem((blocks, rows, C), BF16),
        vmem((blocks, ny, rows1, C), BF16),
        vmem((blocks, ny, rows1, C), BF16),
        vmem((rows1, C), F32),
        vmem((blocks, nz, rows2, C), F32),
        vmem((nx * nz, rows2, C), F32),
        vmem((nz, rows2, C), F32),
        vmem((2, ny, rows1, C), BF16),
        dma((6,)),
        dma((wh // 2,)),
        dma((3 * nz,)),
        dma((wh // 2,)),
        dma((3 * nz,)),
        dma((2,)),
        dma((blocks, 2)),
        dma((blocks + 1, 2)),
        dma((nx, 2)),
        dma((nx, 2)),
        dma((blocks, 2)),
        dma((blocks, 2)),
        dma((blocks, 2)),
        dma((2,)),
        dma((ny, 2)),
        dma((2,)),
    ]
    grads, grad_video = pl.pallas_call(
        functools.partial(kernel, nx, ny, nz, 1.0 / float(pixels) ** 0.5),
        out_shape=(
            jax.ShapeDtypeStruct((2, ny, rows1, C), BF16),
            jax.ShapeDtypeStruct(tile, BF16),
        ),
        in_specs=[pl.BlockSpec(memory_space=pl.ANY)] * 4,
        out_specs=(pl.BlockSpec(memory_space=vmem),) * 2,
        scratch_shapes=scratch,
        compiler_params=pltpu.CompilerParams(
            collective_id=0, has_side_effects=True, vmem_limit_bytes=60 << 20
        ),
    )(video, cotangent, spatial_weights, temporal_weights)
    grads = grads.reshape(1, 12, C, C).astype(F32)
    return grads[:, :9], grads[:, 9:], grad_video


def solution(mesh):
    nx = mesh.shape["section"]
    space = mesh.shape["space"]
    nz = 1 << ((space.bit_length() - 1 + 1) // 2)
    ny = space // nz
    frames = 2 * mesh.shape["tm"]
    height = 2 * nx * space
    pixels = frames * height * C
    tiles = P("tm", ("section", "space"), None, None)
    owned = P("section", None, None, None)
    return jax.shard_map(
        functools.partial(on_device, nx, ny, nz, pixels),
        mesh=mesh,
        in_specs=(tiles, tiles, owned, owned),
        out_specs=(owned, owned, tiles),
        check_vma=False,
    )
```
